32 devices in a mesh: dp: 4 (over x, core), blk: 4 (over z), inner: 2 (over y).
Axes of the slice: x: 2, y: 2, z: 4, core: 2. Of those that a mesh axis runs over, the one named last changes fastest.
Arguments:
- queries: bfloat16 [4, 1024, 1536], P('dp', ('blk', 'inner')), may hold values from -6 to 6
- keys: bfloat16 [4, 1024, 1536], P('dp', ('blk', 'inner')), may hold values from -6 to 6
- values: bfloat16 [4, 1024, 1536], P('dp', ('blk', 'inner')), may hold values from -6 to 6
- v_scale: bfloat16 [4, 1024, 12], P('dp', ('blk', 'inner')), may hold values from 0.5 to 2
- d_out: bfloat16 [4, 1024, 1536], P('dp', ('blk', 'inner')), may hold values from -45 to 45
- q_gain: float32 [128], replicated, may hold values from 0.1 to 1.9
- k_gain: float32 [128], replicated, may hold values from 0.1 to 1.9
- segment_ids: int32 [4, 1024], P('dp'), may hold values from 0 to 63, never falling along the last dimension, each value on 1 to 32 neighbouring positions
Outputs:
- attended: bfloat16 [4, 1024, 1536], P('dp', ('blk', 'inner'))
- d_queries: bfloat16 [4, 1024, 1536], P('dp', ('blk', 'inner'))
- d_keys: bfloat16 [4, 1024, 1536], P('dp', ('blk', 'inner'))
- d_values: bfloat16 [4, 1024, 1536], P('dp', ('blk', 'inner'))
- d_q_gain: float32 [128], replicated
- d_k_gain: float32 [128], replicated
The draws below stay inside these ranges and needn't reach their ends.
Inputs may be any that keep to these rules, and one draw needn't show every extreme that they name: `segment_ids`: segment numbers never fall along a sequence; every segment has between 1 and 32 tokens and some segment has exactly 32.
All inputs are finite; a program needn't handle non-finite values.
Results may differ from the reference program's by a relative error of at most 0.0086.
Values may be sent and summed in bfloat16 or wider, within the bound.
A program may use at most 64 MiB of HBM per device.

```python
import math
import jax
import jax.numpy as jnp
import numpy as np
from jax import lax

HEADS = 12
HD = 128
SEQS = 4
BLOCK = 256
HALO = 32
S = 1024
N_BLK = 4


def draw_d_out(key, part):
    normal_part = jnp.clip(jax.random.normal(key, (SEQS, S, HEADS * HD), jnp.float32), -5.0, 5.0)
    rise_tokens = 1.0 + 2.0 * jnp.arange(S, dtype=jnp.float32) / (S - 1)
    rise_seqs = 1.0 + 2.0 * jnp.arange(SEQS, dtype=jnp.float32) / max(SEQS - 1, 1)
    return (normal_part * rise_tokens[None, :, None] * rise_seqs[:, None, None]).astype(jnp.bfloat16)


def level_of(key, extent, split, least, largest):
    factor_of = 1.0
    for dim, blocks in split:
        draws = jax.random.uniform(jax.random.fold_in(jax.random.fold_in(key, 6), dim), (blocks,), jnp.float32, least / len(split), largest / len(split))
        factor_of = factor_of * jnp.repeat(jnp.exp(draws), extent[dim] // blocks).reshape((-1,) + (1,) * (len(extent) - 1 - dim))
    return factor_of


def split_up(number_of, total, limit, lean):
    portions = [(1 << 20) // math.isqrt(standing ** lean) + 1 for standing in range(2, number_of + 1)]
    rest, holding = total - limit - (number_of - 1), [1] * (number_of - 1)
    while rest > 0:
        candidates = [i for i in range(number_of - 1) if holding[i] < limit]
        whole, budget = sum([portions[i] for i in candidates]), rest
        for i in candidates:
            extra = min(limit - holding[i], max(1, budget * portions[i] // whole), rest)
            holding[i] = holding[i] + extra
            rest = rest - extra
    return np.array([limit] + holding)


def ragged_sizes(stream_key, amount, total, most, skew):
    if amount == 2:
        one = jax.random.randint(stream_key, (), max(1, total - most), min(most, total - 1) + 1)
        return jnp.stack([one, total - one])
    tallies = jnp.asarray(split_up(amount, total, most, skew), jnp.int32)
    twos = (amount - 1) // 2
    donor, receiver = tallies[1:1 + 2 * twos:2], tallies[2:2 + 2 * twos:2]
    margin = jnp.minimum(donor - 1, most - receiver)
    shifted = jax.random.randint(jax.random.fold_in(stream_key, 1), (twos,), 0, 1 << 20) % (margin + 1)
    tallies = tallies.at[1:1 + 2 * twos:2].set(donor - shifted).at[2:2 + 2 * twos:2].set(receiver + shifted)
    return tallies[jax.random.permutation(jax.random.fold_in(stream_key, 2), amount)]


def noise(rng, dims, scale, bound, cuts=(), kind=jnp.bfloat16):
    entries = jax.random.normal(rng, dims, jnp.float32) * scale
    if len(cuts) > 0:
        entries = level_of(rng, dims, cuts, -0.22, 0.18) * entries
    return jnp.clip(entries, min=-bound, max=bound).astype(kind)


def setup_inputs(seed: int = 0) -> dict:
    splits = jax.random.split(jax.random.key(seed), 9)
    return {
        "queries": noise(splits[0], (SEQS, S, HEADS * HD), 1.0, 6.0, ((0, 4), (1, 8))),
        "keys": noise(splits[1], (SEQS, S, HEADS * HD), 1.0, 6.0, ((0, 4), (1, 8))),
        "values": noise(splits[2], (SEQS, S, HEADS * HD), 1.0, 6.0, ((0, 4), (1, 8))),
        "v_scale": jnp.clip(jnp.exp(math.log(2.0) - 1.3862944 * jax.random.uniform(splits[3], (SEQS, S, HEADS), jnp.float32) ** level_of(splits[3], (SEQS, S, HEADS), ((0, 4), (1, 8)), -0.2, 0.2)), 0.5, 2.0).astype(jnp.bfloat16),
        "d_out": draw_d_out(jax.random.fold_in(splits[8], 71), 0),
        "q_gain": jnp.clip(1.0 + 0.18 * jax.random.normal(splits[5], (HD,), jnp.float32), 0.1, 1.9),
        "k_gain": jnp.clip(1.0 + 0.18 * jax.random.normal(splits[6], (HD,), jnp.float32), 0.1, 1.9),
        "segment_ids": jax.vmap(lambda own: jnp.searchsorted(jnp.cumsum(ragged_sizes(own, 16 * N_BLK, S, HALO, 2)), jnp.arange(S), side="right"))(jax.random.split(splits[7], SEQS)).reshape((SEQS, S)).astype(jnp.int32),
    }


EPSILON = 1e-06

def normalize(raw_values, gain_vector):
    as_float = raw_values.astype(jnp.float32)
    inverse = lax.rsqrt(lax.optimization_barrier(jnp.mean(as_float * as_float, axis=-1, keepdims=True)) + EPSILON)
    unit_rows = as_float * inverse
    return ((unit_rows * gain_vector).astype(jnp.bfloat16), unit_rows, inverse)

def norm_back(d_norm, unit_rows, inverse, gain_vector):
    d_unit = d_norm * gain_vector
    d_raw = inverse * (d_unit - unit_rows * lax.optimization_barrier(jnp.mean(d_unit * unit_rows, axis=-1, keepdims=True)))
    return (d_raw, lax.optimization_barrier(jnp.sum(d_norm * unit_rows, axis=(0, 1))))

def reference(queries, keys, values, v_scale, d_out, q_gain, k_gain, segment_ids):
    head_shape = (S, HEADS, HD)
    score_scale = 1.0 / math.sqrt(HD)

    def scores_of(q_rows, k_rows, seg_query, seg_key):
        scores = jnp.einsum('qhd,khd->hqk', q_rows.astype(jnp.float32), k_rows.astype(jnp.float32)) * score_scale
        seg_match = (seg_query[:, None] == seg_key[None, :])[None]
        return (scores, seg_match)

    def one_sequence(operands):
        q_raw, k_raw, v_raw, v_scl, grad_raw, segments = operands
        q_norm, q_unit, q_inv = normalize(q_raw.reshape(head_shape), q_gain)
        k_norm, k_unit, k_inv = normalize(k_raw.reshape(head_shape), k_gain)
        scale_f = v_scl.astype(jnp.float32)[:, :, None]
        v_deq = (v_raw.reshape(head_shape).astype(jnp.float32) * scale_f).astype(jnp.bfloat16)
        grad_out = grad_raw.reshape(head_shape)
        pad_rows = ((BLOCK, BLOCK), (0, 0), (0, 0))
        q_pad = jnp.pad(q_norm, pad_rows)
        k_pad = jnp.pad(k_norm, pad_rows)
        v_pad = jnp.pad(v_deq, pad_rows)
        grad_pad = jnp.pad(grad_out, pad_rows)
        segment_pad = jnp.pad(segments, (BLOCK, BLOCK), constant_values=-1)
        block_ids = jnp.arange(N_BLK, dtype=jnp.int32)

        def forward_block(block_index):
            row_start = (block_index * BLOCK).astype(jnp.int32)
            q_rows = lax.dynamic_slice_in_dim(q_norm, row_start, BLOCK, 0)
            seg_query = lax.dynamic_slice_in_dim(segments, row_start, BLOCK, 0)
            k_rows = lax.dynamic_slice_in_dim(k_pad, row_start, 3 * BLOCK, 0)
            v_rows = lax.dynamic_slice_in_dim(v_pad, row_start, 3 * BLOCK, 0)
            seg_key = lax.dynamic_slice_in_dim(segment_pad, row_start, 3 * BLOCK, 0)
            scores, seg_match = scores_of(q_rows, k_rows, seg_query, seg_key)
            summed = lax.optimization_barrier(jnp.sum(jnp.where(seg_match, jnp.exp(scores), 0.0), axis=2))
            log_total = jnp.log(summed)
            weights = jnp.where(seg_match, jnp.exp(scores - log_total[:, :, None]), 0.0)
            out_rows = jnp.einsum('hqk,khd->qhd', weights.astype(jnp.bfloat16).astype(jnp.float32), v_rows.astype(jnp.float32))
            return (out_rows.astype(jnp.bfloat16), log_total)
        out_blocks, total_blocks = lax.map(forward_block, block_ids)
        attended = out_blocks.reshape(head_shape)
        log_total = jnp.transpose(total_blocks, (1, 0, 2)).reshape(HEADS, S)
        out_dot = lax.optimization_barrier(jnp.sum(grad_out.astype(jnp.float32) * attended.astype(jnp.float32), axis=-1)).T
        total_pad = jnp.pad(log_total, ((0, 0), (BLOCK, BLOCK)))
        dot_pad = jnp.pad(out_dot, ((0, 0), (BLOCK, BLOCK)))

        def query_block(block_index):
            row_start = (block_index * BLOCK).astype(jnp.int32)
            q_rows = lax.dynamic_slice_in_dim(q_norm, row_start, BLOCK, 0)
            grad_rows = lax.dynamic_slice_in_dim(grad_out, row_start, BLOCK, 0)
            seg_query = lax.dynamic_slice_in_dim(segments, row_start, BLOCK, 0)
            total_rows = lax.dynamic_slice_in_dim(log_total, row_start, BLOCK, 1)
            dot_rows = lax.dynamic_slice_in_dim(out_dot, row_start, BLOCK, 1)
            k_rows = lax.dynamic_slice_in_dim(k_pad, row_start, 3 * BLOCK, 0)
            v_rows = lax.dynamic_slice_in_dim(v_pad, row_start, 3 * BLOCK, 0)
            seg_key = lax.dynamic_slice_in_dim(segment_pad, row_start, 3 * BLOCK, 0)
            scores, seg_match = scores_of(q_rows, k_rows, seg_query, seg_key)
            weights = jnp.where(seg_match, jnp.exp(scores - total_rows[:, :, None]), 0.0)
            d_weights = jnp.einsum('qhd,khd->hqk', grad_rows.astype(jnp.float32), v_rows.astype(jnp.float32))
            d_scores = (weights * (d_weights - dot_rows[:, :, None])).astype(jnp.bfloat16)
            return score_scale * jnp.einsum('hqk,khd->qhd', d_scores.astype(jnp.float32), k_rows.astype(jnp.float32))

        def key_block(block_index):
            row_start = (block_index * BLOCK).astype(jnp.int32)
            k_rows = lax.dynamic_slice_in_dim(k_norm, row_start, BLOCK, 0)
            v_rows = lax.dynamic_slice_in_dim(v_deq, row_start, BLOCK, 0)
            seg_key = lax.dynamic_slice_in_dim(segments, row_start, BLOCK, 0)
            q_rows = lax.dynamic_slice_in_dim(q_pad, row_start, 3 * BLOCK, 0)
            grad_rows = lax.dynamic_slice_in_dim(grad_pad, row_start, 3 * BLOCK, 0)
            seg_query = lax.dynamic_slice_in_dim(segment_pad, row_start, 3 * BLOCK, 0)
            total_rows = lax.dynamic_slice_in_dim(total_pad, row_start, 3 * BLOCK, 1)
            dot_rows = lax.dynamic_slice_in_dim(dot_pad, row_start, 3 * BLOCK, 1)
            scores, seg_match = scores_of(q_rows, k_rows, seg_query, seg_key)
            weights = jnp.where(seg_match, jnp.exp(scores - total_rows[:, :, None]), 0.0)
            d_weights = jnp.einsum('qhd,khd->hqk', grad_rows.astype(jnp.float32), v_rows.astype(jnp.float32))
            d_scores = (weights * (d_weights - dot_rows[:, :, None])).astype(jnp.bfloat16)
            d_key = score_scale * jnp.einsum('hqk,qhd->khd', d_scores.astype(jnp.float32), q_rows.astype(jnp.float32))
            d_val = jnp.einsum('hqk,qhd->khd', weights.astype(jnp.bfloat16).astype(jnp.float32), grad_rows.astype(jnp.float32))
            return (d_key, d_val)
        dq_norm = lax.map(query_block, block_ids).reshape(head_shape)
        dk_blocks, dv_blocks = lax.map(key_block, block_ids)
        dk_norm = dk_blocks.reshape(head_shape)
        dv_deq = dv_blocks.reshape(head_shape)
        d_q_raw, gain_q = norm_back(dq_norm, q_unit, q_inv, q_gain)
        d_k_raw, gain_k = norm_back(dk_norm, k_unit, k_inv, k_gain)
        d_val_raw = (dv_deq * scale_f).astype(jnp.bfloat16)
        flat_shape = (S, HEADS * HD)
        return (attended.reshape(flat_shape), d_q_raw.astype(jnp.bfloat16).reshape(flat_shape), d_k_raw.astype(jnp.bfloat16).reshape(flat_shape), d_val_raw.reshape(flat_shape), gain_q, gain_k)
    results = lax.map(one_sequence, (queries, keys, values, v_scale, d_out, segment_ids))
    return (results[0], results[1], results[2], results[3], lax.optimization_barrier(jnp.sum(results[4], axis=0)), lax.optimization_barrier(jnp.sum(results[5], axis=0)))
```

```python
import functools
import math

import jax
import jax.numpy as jnp
from jax import lax
from jax.experimental import pallas as pl
from jax.experimental.pallas import tpu as pltpu
from jax.sharding import PartitionSpec as P

EPSILON = 1e-06
MESH = pl.DeviceIdType.MESH
AXES = ("dp", "blk", "inner")
F32 = jnp.float32
BF16 = jnp.bfloat16
NT = (((1,), (1,)), ((), ()))
NN = (((1,), (0,)), ((), ()))
TN = (((0,), (0,)), ((), ()))


def dot(a, b, dims):
    return lax.dot_general(a, b, dims, preferred_element_type=F32)


def unit(x):
    inverse = lax.rsqrt(jnp.mean(x * x, axis=-1, keepdims=True) + EPSILON)
    return x * inverse, inverse


def norm_back(d_norm, unit_rows, inverse, gain):
    d_unit = d_norm * gain
    mean = jnp.mean(d_unit * unit_rows, axis=-1, keepdims=True)
    return inverse * (d_unit - unit_rows * mean)


def attend(q_norm, k_norm, v_deq, grad, same, scale):
    e = jnp.where(same, jnp.exp(dot(k_norm, q_norm, NT) * scale), 0.0)
    w = e * (1.0 / jnp.sum(e, axis=0, keepdims=True))
    w_b = w.astype(BF16)
    d_w = dot(v_deq, grad, NT)
    out_dot = jnp.sum(w * d_w, axis=0, keepdims=True)
    d_s = (w * (d_w - out_dot)).astype(BF16)
    return (
        dot(w_b, v_deq, TN),
        dot(d_s, k_norm, TN) * scale,
        dot(d_s, q_norm, NN) * scale,
        dot(w_b, grad, NN),
    )


def to_column(row):
    n = row.shape[1]
    r = lax.broadcasted_iota(jnp.int32, (n, n), 0)
    c = lax.broadcasted_iota(jnp.int32, (n, n), 1)
    return jnp.sum(jnp.where(r == c, row, 0.0), axis=1, keepdims=True)


def kernel(cfg, q_hbm, k_hbm, v_hbm, s_ref, g_hbm, qg_ref, kg_ref, seg_ref,
           att_o, dq_o, dk_o, dv_o, gq_o, gk_o,
           qv, kv, vv, gv, vd, halo, gsrc, gslot,
           load_sem, send_sem, recv_sem, gsend, grecv):
    sizes, rows, heads, hd, h, hpc = cfg
    n_dp, n_blk, n_inner = sizes
    nc = heads // hpc
    width = hpc * hd
    scale = 1.0 / math.sqrt(hd)
    blk, inner = lax.axis_index("blk"), lax.axis_index("inner")
    p = blk * n_inner + inner
    last = n_blk * n_inner - 1
    has_left, has_right = p > 0, p < last
    left, right = p - 1, p + 1

    def at(pos):
        return {"blk": pos // n_inner, "inner": lax.rem(pos, n_inner)}

    loads = [
        pltpu.make_async_copy(src, dst, load_sem.at[i])
        for i, (src, dst) in enumerate(((v_hbm, vv), (q_hbm, qv), (k_hbm, kv), (g_hbm, gv)))
    ]
    for c in loads:
        c.start()

    barrier = pltpu.get_barrier_semaphore()
    for axis, n in zip(AXES, sizes):
        me = lax.axis_index(axis)
        for d in range(1, n):
            pl.semaphore_signal(barrier, inc=1, device_id={axis: lax.rem(me + d, n)},
                                device_id_type=MESH)

    @pl.when(has_left)
    def _():
        pl.semaphore_signal(barrier, inc=1, device_id=at(left), device_id_type=MESH)

    @pl.when(has_right)
    def _():
        pl.semaphore_signal(barrier, inc=1, device_id=at(right), device_id_type=MESH)

    lane = lax.broadcasted_iota(jnp.int32, (rows, heads), 1)
    s_f = s_ref[...].astype(F32)

    def scale_of(head):
        return jnp.sum(jnp.where(lane == head, s_f, 0.0), axis=1, keepdims=True)

    loads[0].wait()
    for head in range(heads):
        cols = slice(head * hd, (head + 1) * hd)
        vd[:, cols] = (vv[:, cols].astype(F32) * s_f[:, head:head + 1]).astype(BF16)

    def seg_at(pos):
        start = pl.multiple_of(pos * rows, 128)
        return seg_ref[:, pl.ds(start, rows)].astype(F32)

    own = seg_at(p)
    prev = jnp.where(has_left, seg_at(jnp.maximum(left, 0)), -1.0)
    nxt = jnp.where(has_right, seg_at(jnp.minimum(right, last)), -2.0)
    own_col = to_column(own)
    edge = jnp.concatenate(
        [prev[:, rows - h:], own[:, :h], own[:, rows - h:], nxt[:, :h]], axis=1)
    edge_col = to_column(edge)
    same_own = own_col == own
    same_edge = edge_col == edge
    before = jnp.sum(prev[:, rows - 1:], axis=1, keepdims=True)
    after = jnp.sum(nxt[:, :1], axis=1, keepdims=True)
    inside = jnp.where((own_col == before) | (own_col == after), 0.0, 1.0)
    split_lo = own_col[:h] == before
    split_hi = own_col[rows - h:] == after
    split_f = 1.0 - jnp.concatenate([inside[:h], inside[rows - h:]], axis=0)

    pl.semaphore_wait(barrier, sum(sizes) - len(sizes)
                      + has_left.astype(jnp.int32) + has_right.astype(jnp.int32))

    srcs = (k_hbm, q_hbm, vd, g_hbm)

    def remote(side, i, c):
        if isinstance(c, int):
            cols = slice(c * width, (c + 1) * width)
        else:
            cols = pl.ds(pl.multiple_of(c * width, 128), width)
        own_rows = slice(0, h) if side == 0 else slice(rows - h, rows)
        return pltpu.make_async_remote_copy(
            src_ref=srcs[i].at[own_rows, cols],
            dst_ref=halo.at[i, 1 - side, :, cols],
            send_sem=send_sem.at[side, i, c],
            recv_sem=recv_sem.at[1 - side, i, c],
            device_id=at(left if side == 0 else right),
            device_id_type=MESH,
        )

    def receive(side, i, c):
        cols = pl.ds(pl.multiple_of(c * width, 128), width)
        return pltpu.make_async_remote_copy(
            src_ref=halo.at[i, side, :, cols],
            dst_ref=halo.at[i, side, :, cols],
            send_sem=send_sem.at[side, i, c],
            recv_sem=recv_sem.at[side, i, c],
            device_id=at(left if side == 0 else right),
            device_id_type=MESH,
        )

    sides = ((0, has_left), (1, has_right))
    for c in range(nc):
        for side, there in sides:
            @pl.when(there)
            def _():
                for i in range(4):
                    remote(side, i, c).start()

    for side, there in sides:
        @pl.when(jnp.logical_not(there))
        def _():
            halo[:, side] = jnp.zeros((4, h, heads * hd), BF16)

    q_gain, k_gain = qg_ref[...], kg_ref[...]
    for c in loads[1:]:
        c.wait()

    def own_step(c, acc):
        acc_q, acc_k = acc
        for j in range(hpc):
            head = c * hpc + j
            cols = pl.ds(pl.multiple_of(head * hd, 128), hd)
            q_unit, q_inv = unit(qv[:, cols].astype(F32))
            k_unit, k_inv = unit(kv[:, cols].astype(F32))
            out, d_q, d_k, d_v = attend(
                (q_unit * q_gain).astype(BF16), (k_unit * k_gain).astype(BF16),
                vd[:, cols], gv[:, cols], same_own, scale)
            att_o[:, cols] = out.astype(BF16)
            dq_o[:, cols] = norm_back(d_q, q_unit, q_inv, q_gain).astype(BF16)
            dk_o[:, cols] = norm_back(d_k, k_unit, k_inv, k_gain).astype(BF16)
            dv_o[:, cols] = (d_v * scale_of(head)).astype(BF16)
            acc_q = acc_q + jnp.sum(d_q * q_unit * inside, axis=0, keepdims=True)
            acc_k = acc_k + jnp.sum(d_k * k_unit * inside, axis=0, keepdims=True)
        return acc_q, acc_k

    zero = jnp.zeros((1, hd), F32)
    acc = lax.fori_loop(0, nc, own_step, (zero, zero))

    def joined(i, ref, cols):
        return jnp.concatenate(
            [halo[i, 0, :, cols], ref[0:h, cols], ref[rows - h:rows, cols], halo[i, 1, :, cols]],
            axis=0)

    def put(ref, cols, value):
        ref[0:h, cols] = jnp.where(split_lo, value[:h].astype(F32),
                                   ref[0:h, cols].astype(F32)).astype(BF16)
        ref[rows - h:rows, cols] = jnp.where(split_hi, value[h:].astype(F32),
                                             ref[rows - h:rows, cols].astype(F32)).astype(BF16)

    def edge_step(c, acc):
        acc_q, acc_k = acc
        for side, there in sides:
            @pl.when(there)
            def _():
                for i in range(4):
                    receive(side, i, c).wait_recv()
        for j in range(hpc):
            head = c * hpc + j
            cols = pl.ds(pl.multiple_of(head * hd, 128), hd)
            q_unit, q_inv = unit(joined(1, qv, cols).astype(F32))
            k_unit, k_inv = unit(joined(0, kv, cols).astype(F32))
            out, d_q, d_k, d_v = attend(
                (q_unit * q_gain).astype(BF16), (k_unit * k_gain).astype(BF16),
                joined(2, vd, cols), joined(3, gv, cols), same_edge, scale)
            mid = slice(h, 3 * h)
            d_q, d_k, q_unit, k_unit = d_q[mid], d_k[mid], q_unit[mid], k_unit[mid]
            s_all = scale_of(head)
            s_mid = jnp.concatenate([s_all[:h], s_all[rows - h:]], axis=0)
            put(att_o, cols, out[mid])
            put(dq_o, cols, norm_back(d_q, q_unit, q_inv[mid], q_gain))
            put(dk_o, cols, norm_back(d_k, k_unit, k_inv[mid], k_gain))
            put(dv_o, cols, d_v[mid] * s_mid)
            acc_q = acc_q + jnp.sum(jnp.where(split_f > 0.5, d_q * q_unit, 0.0), axis=0, keepdims=True)
            acc_k = acc_k + jnp.sum(jnp.where(split_f > 0.5, d_k * k_unit, 0.0), axis=0, keepdims=True)
        return acc_q, acc_k

    acc_q, acc_k = lax.fori_loop(0, nc, edge_step, acc)

    row = lax.broadcasted_iota(jnp.int32, (8, hd), 0)
    total = jnp.where(row == 0, acc_q, jnp.where(row == 1, acc_k, 0.0))
    offset = 0
    for stage, (axis, n) in enumerate(zip(AXES, sizes)):
        me = lax.axis_index(axis)
        gsrc[stage] = total
        gslot[offset + me] = total

        def gain_copy(d, slot, to):
            return pltpu.make_async_remote_copy(
                src_ref=gsrc.at[stage], dst_ref=gslot.at[offset + slot],
                send_sem=gsend.at[offset + d], recv_sem=grecv.at[offset + d],
                device_id={axis: to}, device_id_type=MESH)

        for d in range(1, n):
            gain_copy(d, me, lax.rem(me + d, n)).start()
        for d in range(1, n):
            gain_copy(d, lax.rem(me - d + n, n), lax.rem(me + d, n)).wait()
        total = gslot[offset]
        for i in range(1, n):
            total = total + gslot[offset + i]
        offset += n
    gq_o[...] = total[0:1]
    gk_o[...] = total[1:2]

    for c in range(nc):
        for side, there in sides:
            @pl.when(there)
            def _():
                for i in range(4):
                    remote(side, i, c).wait_send()


def local(queries, keys, values, v_scale, d_out, q_gain, k_gain, segment_ids):
    _, rows, cols = queries.shape
    hd = q_gain.shape[0]
    heads = cols // hd
    sizes = tuple(lax.axis_size(a) for a in AXES)
    h = rows * sizes[2] // 8
    hpc = 3 if heads % 3 == 0 else 1
    nc = heads // hpc
    flat = lambda x: x.reshape(rows, x.shape[2])
    vmem = pl.BlockSpec(memory_space=pltpu.VMEM)
    hbm = pl.BlockSpec(memory_space=pl.ANY)
    big = jax.ShapeDtypeStruct((rows, cols), BF16)
    small = jax.ShapeDtypeStruct((1, hd), F32)
    slots = sum(sizes)
    outs = pl.pallas_call(
        functools.partial(kernel, (sizes, rows, heads, hd, h, hpc)),
        out_shape=(big, big, big, big, small, small),
        in_specs=[hbm, hbm, hbm, vmem, hbm, vmem, vmem, vmem],
        out_specs=(vmem,) * 6,
        scratch_shapes=[
            pltpu.VMEM((rows, cols), BF16),
            pltpu.VMEM((rows, cols), BF16),
            pltpu.VMEM((rows, cols), BF16),
            pltpu.VMEM((rows, cols), BF16),
            pltpu.VMEM((rows, cols), BF16),
            pltpu.VMEM((4, 2, h, cols), BF16),
            pltpu.VMEM((3, 8, hd), F32),
            pltpu.VMEM((slots, 8, hd), F32),
            pltpu.SemaphoreType.DMA((4,)),
            pltpu.SemaphoreType.DMA((2, 4, nc)),
            pltpu.SemaphoreType.DMA((2, 4, nc)),
            pltpu.SemaphoreType.DMA((slots,)),
            pltpu.SemaphoreType.DMA((slots,)),
        ],
        compiler_params=pltpu.CompilerParams(
            collective_id=0, has_side_effects=True, vmem_limit_bytes=32 << 20),
    )(flat(queries), flat(keys), flat(values), flat(v_scale), flat(d_out),
      q_gain.reshape(1, hd), k_gain.reshape(1, hd), segment_ids)
    wide = tuple(x.reshape(1, rows, cols) for x in outs[:4])
    return wide + (outs[4].reshape(hd), outs[5].reshape(hd))


def solution(mesh):
    tokens = P("dp", ("blk", "inner"), None)
    return jax.shard_map(
        local,
        mesh=mesh,
        in_specs=(tokens,) * 5 + (P(), P(), P("dp", None)),
        out_specs=(tokens,) * 4 + (P(), P()),
        check_vma=False,
    )
```

```python
import functools
import math

import jax
import jax.numpy as jnp
from jax import lax
from jax.experimental import pallas as pl
from jax.experimental.pallas import tpu as pltpu
from jax.sharding import PartitionSpec as P

EPSILON = 1e-06
MESH = pl.DeviceIdType.MESH
AXES = ("dp", "blk", "inner")
F32 = jnp.float32
BF16 = jnp.bfloat16
NT = (((1,), (1,)), ((), ()))
NN = (((1,), (0,)), ((), ()))
TN = (((0,), (0,)), ((), ()))


def dot(a, b, dims):
    return lax.dot_general(a, b, dims, preferred_element_type=F32)


def unit(x):
    inverse = lax.rsqrt(jnp.mean(x * x, axis=-1, keepdims=True) + EPSILON)
    return x * inverse, inverse


def norm_back(d_norm, unit_rows, inverse, gain):
    d_unit = d_norm * gain
    mean = jnp.mean(d_unit * unit_rows, axis=-1, keepdims=True)
    return inverse * (d_unit - unit_rows * mean)


def attend(q_norm, k_norm, v_deq, grad, same, scale):
    e = jnp.where(same, jnp.exp(dot(k_norm, q_norm, NT) * scale), 0.0)
    w = e * (1.0 / jnp.sum(e, axis=0, keepdims=True))
    w_b = w.astype(BF16)
    d_w = dot(v_deq, grad, NT)
    out_dot = jnp.sum(w * d_w, axis=0, keepdims=True)
    d_s = (w * (d_w - out_dot)).astype(BF16)
    return (
        dot(w_b, v_deq, TN),
        dot(d_s, k_norm, TN) * scale,
        dot(d_s, q_norm, NN) * scale,
        dot(w_b, grad, NN),
    )


def to_column(row):
    n = row.shape[1]
    r = lax.broadcasted_iota(jnp.int32, (n, n), 0)
    c = lax.broadcasted_iota(jnp.int32, (n, n), 1)
    return jnp.sum(jnp.where(r == c, row, 0.0), axis=1, keepdims=True)


def transposed(x):
    n = x.shape[1]
    r = lax.broadcasted_iota(jnp.int32, (n, n), 0)
    c = lax.broadcasted_iota(jnp.int32, (n, n), 1)
    return dot((r == c).astype(F32).astype(BF16), x, NT)


def store(*refs):
    n = len(refs) // 2
    sem = refs[-1]
    copies = [pltpu.make_async_copy(refs[i], refs[n + i], sem.at[i]) for i in range(n)]
    for c in copies:
        c.start()
    for c in copies:
        c.wait()


def grouped(sizes):
    groups = []
    for axis, n in zip(AXES, sizes):
        if groups and groups[-1][1] * n <= 32:
            groups[-1] = (groups[-1][0] + (axis,), groups[-1][1] * n)
        else:
            groups.append(((axis,), n))
    return groups


def kernel(cfg, q_hbm, k_hbm, v_hbm, s_hbm, g_hbm, qg_hbm, kg_hbm, seg_hbm,
           att_o, dq_o, dk_o, dv_o, gq_o, gk_o,
           qv, kv, vv, gv, s_ref, qg_ref, kg_ref, seg_ref, vd, halo, gsrc, gslot,
           load_sem, send_sem, recv_sem, gsend, grecv):
    sizes, rows, heads, hd, h, hpc = cfg
    n_dp, n_blk, n_inner = sizes
    nc = heads // hpc
    width = hpc * hd
    scale = 1.0 / math.sqrt(hd)
    blk, inner = lax.axis_index("blk"), lax.axis_index("inner")
    p = blk * n_inner + inner
    last = n_blk * n_inner - 1
    has_left, has_right = p > 0, p < last
    left, right = p - 1, p + 1

    size_of = dict(zip(AXES, sizes))
    stages = grouped(sizes)

    def place(axes):
        index = 0
        for axis in axes:
            index = index * size_of[axis] + lax.axis_index(axis)
        return index

    def member(axes, index):
        device = {}
        for axis in reversed(axes):
            device[axis] = lax.rem(index, size_of[axis])
            index = index // size_of[axis]
        return device

    def at(pos):
        return {"blk": pos // n_inner, "inner": lax.rem(pos, n_inner)}

    loads = [
        pltpu.make_async_copy(src, dst, load_sem.at[i])
        for i, (src, dst) in enumerate(((s_hbm, s_ref), (v_hbm, vv), (seg_hbm, seg_ref), (qg_hbm, qg_ref),
                                   (kg_hbm, kg_ref), (q_hbm, qv), (k_hbm, kv), (g_hbm, gv)))
    ]
    for c in loads:
        c.start()

    barrier = pltpu.get_barrier_semaphore()
    for axes, n in stages:
        me = place(axes)
        for d in range(1, n):
            pl.semaphore_signal(barrier, inc=1, device_id=member(axes, lax.rem(me + d, n)),
                                device_id_type=MESH)

    @pl.when(has_left)
    def _():
        pl.semaphore_signal(barrier, inc=1, device_id=at(left), device_id_type=MESH)

    @pl.when(has_right)
    def _():
        pl.semaphore_signal(barrier, inc=1, device_id=at(right), device_id_type=MESH)

    lane = lax.broadcasted_iota(jnp.int32, (rows, heads), 1)
    loads[0].wait()
    s_f = transposed(s_ref[...])

    def scale_of(head):
        return jnp.sum(jnp.where(lane == head, s_f, 0.0), axis=1, keepdims=True)

    loads[1].wait()
    for head in range(heads):
        cols = slice(head * hd, (head + 1) * hd)
        vd[:, cols] = (vv[:, cols].astype(F32) * s_f[:, head:head + 1]).astype(BF16)

    def seg_at(pos):
        start = pl.multiple_of(pos * rows, 128)
        return seg_ref[:, pl.ds(start, rows)].astype(F32)

    loads[2].wait()
    own = seg_at(p)
    prev = jnp.where(has_left, seg_at(jnp.maximum(left, 0)), -1.0)
    nxt = jnp.where(has_right, seg_at(jnp.minimum(right, last)), -2.0)
    own_col = to_column(own)
    edge = jnp.concatenate(
        [prev[:, rows - h:], own[:, :h], own[:, rows - h:], nxt[:, :h]], axis=1)
    edge_col = to_column(edge)
    same_own = own_col == own
    same_edge = edge_col == edge
    before = jnp.sum(prev[:, rows - 1:], axis=1, keepdims=True)
    after = jnp.sum(nxt[:, :1], axis=1, keepdims=True)
    inside = jnp.where((own_col == before) | (own_col == after), 0.0, 1.0)
    split_lo = own_col[:h] == before
    split_hi = own_col[rows - h:] == after
    split_f = 1.0 - jnp.concatenate([inside[:h], inside[rows - h:]], axis=0)

    pl.semaphore_wait(barrier, sum(n - 1 for _, n in stages)
                      + has_left.astype(jnp.int32) + has_right.astype(jnp.int32))

    srcs = (k_hbm, q_hbm, vd, g_hbm)

    def remote(side, i, c):
        if isinstance(c, int):
            cols = slice(c * width, (c + 1) * width)
        else:
            cols = pl.ds(pl.multiple_of(c * width, 128), width)
        own_rows = slice(0, h) if side == 0 else slice(rows - h, rows)
        return pltpu.make_async_remote_copy(
            src_ref=srcs[i].at[own_rows, cols],
            dst_ref=halo.at[i, 1 - side, :, cols],
            send_sem=send_sem.at[side, i, c],
            recv_sem=recv_sem.at[1 - side, i, c],
            device_id=at(left if side == 0 else right),
            device_id_type=MESH,
        )

    def receive(side, i, c):
        cols = pl.ds(pl.multiple_of(c * width, 128), width)
        return pltpu.make_async_remote_copy(
            src_ref=halo.at[i, side, :, cols],
            dst_ref=halo.at[i, side, :, cols],
            send_sem=send_sem.at[side, i, c],
            recv_sem=recv_sem.at[side, i, c],
            device_id=at(left if side == 0 else right),
            device_id_type=MESH,
        )

    sides = ((0, has_left), (1, has_right))
    for c in range(nc):
        for side, there in sides:
            @pl.when(there)
            def _():
                for i in range(4):
                    remote(side, i, c).start()

    for side, there in sides:
        @pl.when(jnp.logical_not(there))
        def _():
            halo[:, side] = jnp.zeros((4, h, heads * hd), BF16)

    for c in loads[3:]:
        c.wait()
    q_gain, k_gain = qg_ref[...], kg_ref[...]

    def own_step(c, acc):
        acc_q, acc_k = acc
        for j in range(hpc):
            head = c * hpc + j
            cols = pl.ds(pl.multiple_of(head * hd, 128), hd)
            q_unit, q_inv = unit(qv[:, cols].astype(F32))
            k_unit, k_inv = unit(kv[:, cols].astype(F32))
            out, d_q, d_k, d_v = attend(
                (q_unit * q_gain).astype(BF16), (k_unit * k_gain).astype(BF16),
                vd[:, cols], gv[:, cols], same_own, scale)
            att_o[:, cols] = out.astype(BF16)
            dq_o[:, cols] = norm_back(d_q, q_unit, q_inv, q_gain).astype(BF16)
            dk_o[:, cols] = norm_back(d_k, k_unit, k_inv, k_gain).astype(BF16)
            dv_o[:, cols] = (d_v * scale_of(head)).astype(BF16)
            acc_q = acc_q + jnp.sum(d_q * q_unit * inside, axis=0, keepdims=True)
            acc_k = acc_k + jnp.sum(d_k * k_unit * inside, axis=0, keepdims=True)
        return acc_q, acc_k

    zero = jnp.zeros((1, hd), F32)
    acc = lax.fori_loop(0, nc, own_step, (zero, zero))

    def joined(i, ref, cols):
        return jnp.concatenate(
            [halo[i, 0, :, cols], ref[0:h, cols], ref[rows - h:rows, cols], halo[i, 1, :, cols]],
            axis=0)

    def put(ref, cols, value):
        ref[0:h, cols] = jnp.where(split_lo, value[:h].astype(F32),
                                   ref[0:h, cols].astype(F32)).astype(BF16)
        ref[rows - h:rows, cols] = jnp.where(split_hi, value[h:].astype(F32),
                                             ref[rows - h:rows, cols].astype(F32)).astype(BF16)

    def edge_step(c, acc):
        acc_q, acc_k = acc
        for side, there in sides:
            @pl.when(there)
            def _():
                for i in range(4):
                    receive(side, i, c).wait_recv()
        for j in range(hpc):
            head = c * hpc + j
            cols = pl.ds(pl.multiple_of(head * hd, 128), hd)
            q_unit, q_inv = unit(joined(1, qv, cols).astype(F32))
            k_unit, k_inv = unit(joined(0, kv, cols).astype(F32))
            out, d_q, d_k, d_v = attend(
                (q_unit * q_gain).astype(BF16), (k_unit * k_gain).astype(BF16),
                joined(2, vd, cols), joined(3, gv, cols), same_edge, scale)
            mid = slice(h, 3 * h)
            d_q, d_k, q_unit, k_unit = d_q[mid], d_k[mid], q_unit[mid], k_unit[mid]
            s_all = scale_of(head)
            s_mid = jnp.concatenate([s_all[:h], s_all[rows - h:]], axis=0)
            put(att_o, cols, out[mid])
            put(dq_o, cols, norm_back(d_q, q_unit, q_inv[mid], q_gain))
            put(dk_o, cols, norm_back(d_k, k_unit, k_inv[mid], k_gain))
            put(dv_o, cols, d_v[mid] * s_mid)
            acc_q = acc_q + jnp.sum(jnp.where(split_f > 0.5, d_q * q_unit, 0.0), axis=0, keepdims=True)
            acc_k = acc_k + jnp.sum(jnp.where(split_f > 0.5, d_k * k_unit, 0.0), axis=0, keepdims=True)
        return acc_q, acc_k

    acc_q, acc_k = lax.fori_loop(0, nc, edge_step, acc)

    total = jnp.concatenate([acc_q, acc_k], axis=0)
    offset = 0
    for stage, (axes, n) in enumerate(stages):
        me = place(axes)
        gsrc[stage] = total
        gslot[offset + me] = total

        def gain_copy(d, slot, to):
            return pltpu.make_async_remote_copy(
                src_ref=gsrc.at[stage], dst_ref=gslot.at[offset + slot],
                send_sem=gsend.at[offset + d], recv_sem=grecv.at[offset + d],
                device_id=member(axes, to), device_id_type=MESH)

        for d in range(1, n):
            gain_copy(d, me, lax.rem(me + d, n)).start()
        for d in range(1, n):
            gain_copy(d, lax.rem(me - d + n, n), lax.rem(me + d, n)).wait()
        total = gslot[offset]
        for i in range(1, n):
            total = total + gslot[offset + i]
        offset += n
    gq_o[...] = total[0:1]
    gk_o[...] = total[1:2]

    for c in range(nc):
        for side, there in sides:
            @pl.when(there)
            def _():
                for i in range(4):
                    remote(side, i, c).wait_send()


def local(queries, keys, values, v_scale, d_out, q_gain, k_gain, segment_ids):
    _, rows, cols = queries.shape
    hd = q_gain.shape[0]
    heads = cols // hd
    sizes = tuple(lax.axis_size(a) for a in AXES)
    h = rows * sizes[2] // 8
    hpc = 3 if heads % 3 == 0 else 1
    nc = heads // hpc
    flat = lambda x: x.reshape(rows, x.shape[2])
    vmem = pl.BlockSpec(memory_space=pltpu.VMEM)
    hbm = pl.BlockSpec(memory_space=pltpu.HBM)
    big = jax.ShapeDtypeStruct((rows, cols), BF16)
    small = jax.ShapeDtypeStruct((1, hd), F32)
    slots = sum(n for _, n in grouped(sizes))
    outs = pl.pallas_call(
        functools.partial(kernel, (sizes, rows, heads, hd, h, hpc)),
        out_shape=(big, big, big, big, small, small),
        in_specs=[hbm] * 8,
        out_specs=(vmem,) * 6,
        scratch_shapes=[
            pltpu.VMEM((rows, cols), BF16),
            pltpu.VMEM((rows, cols), BF16),
            pltpu.VMEM((rows, cols), BF16),
            pltpu.VMEM((rows, cols), BF16),
            pltpu.VMEM((heads, rows), BF16),
            pltpu.VMEM((1, hd), F32),
            pltpu.VMEM((1, hd), F32),
            pltpu.VMEM(segment_ids.shape, jnp.int32),
            pltpu.VMEM((rows, cols), BF16),
            pltpu.VMEM((4, 2, h, cols), BF16),
            pltpu.VMEM((3, 2, hd), F32),
            pltpu.VMEM((slots, 2, hd), F32),
            pltpu.SemaphoreType.DMA((8,)),
            pltpu.SemaphoreType.DMA((2, 4, nc)),
            pltpu.SemaphoreType.DMA((2, 4, nc)),
            pltpu.SemaphoreType.DMA((slots,)),
            pltpu.SemaphoreType.DMA((slots,)),
        ],
        compiler_params=pltpu.CompilerParams(
            collective_id=0, has_side_effects=True, vmem_limit_bytes=32 << 20),
    )(*map(lambda x: pltpu.with_memory_space_constraint(x, pltpu.HBM), (flat(queries), flat(keys), flat(values), flat(v_scale).T, flat(d_out),
      q_gain.reshape(1, hd), k_gain.reshape(1, hd), segment_ids)))
    outs = pl.pallas_call(
        store,
        out_shape=(big, big, big, big, small, small),
        in_specs=[vmem] * 6,
        out_specs=(hbm,) * 6,
        scratch_shapes=[pltpu.SemaphoreType.DMA((6,))],
    )(*map(lambda x: pltpu.with_memory_space_constraint(x, pltpu.VMEM), outs))
    wide = tuple(x.reshape(1, rows, cols) for x in outs[:4])
    return wide + (outs[4].reshape(hd), outs[5].reshape(hd))


def solution(mesh):
    tokens = P("dp", ("blk", "inner"), None)
    return jax.shard_map(
        local,
        mesh=mesh,
        in_specs=(tokens,) * 5 + (P(), P(), P("dp", None)),
        out_specs=(tokens,) * 4 + (P(), P()),
        check_vma=False,
    )
```

```python
import functools
import math

import jax
import jax.numpy as jnp
from jax import lax
from jax.experimental import pallas as pl
from jax.experimental.pallas import tpu as pltpu
from jax.sharding import PartitionSpec as P

EPSILON = 1e-06
MESH = pl.DeviceIdType.MESH
AXES = ("dp", "blk", "inner")
F32 = jnp.float32
BF16 = jnp.bfloat16
NT = (((1,), (1,)), ((), ()))
NN = (((1,), (0,)), ((), ()))
TN = (((0,), (0,)), ((), ()))


def dot(a, b, dims):
    return lax.dot_general(a, b, dims, preferred_element_type=F32)


def unit(x):
    inverse = lax.rsqrt(jnp.mean(x * x, axis=-1, keepdims=True) + EPSILON)
    return x * inverse, inverse


def norm_back(d_norm, unit_rows, inverse, gain):
    d_unit = d_norm * gain
    mean = jnp.mean(d_unit * unit_rows, axis=-1, keepdims=True)
    return inverse * (d_unit - unit_rows * mean)


def attend(q_norm, k_norm, v_deq, grad, same, scale):
    e = jnp.where(same, jnp.exp(dot(k_norm, q_norm, NT) * scale), 0.0)
    total = jnp.sum(e, axis=0, keepdims=True)
    w = e * (1.0 / jnp.where(total == 0.0, 1.0, total))
    w_b = w.astype(BF16)
    d_w = dot(v_deq, grad, NT)
    out_dot = jnp.sum(w * d_w, axis=0, keepdims=True)
    d_s = (w * (d_w - out_dot)).astype(BF16)
    return (
        dot(w_b, v_deq, TN),
        dot(d_s, k_norm, TN) * scale,
        dot(d_s, q_norm, NN) * scale,
        dot(w_b, grad, NN),
    )


def to_column(row):
    n = row.shape[1]
    r = lax.broadcasted_iota(jnp.int32, (n, n), 0)
    c = lax.broadcasted_iota(jnp.int32, (n, n), 1)
    return jnp.sum(jnp.where(r == c, row, 0.0), axis=1, keepdims=True)


def transposed(x):
    n = x.shape[1]
    r = lax.broadcasted_iota(jnp.int32, (n, n), 0)
    c = lax.broadcasted_iota(jnp.int32, (n, n), 1)
    return dot((r == c).astype(F32).astype(BF16), x, NT)


def store(*refs):
    n = len(refs) // 2
    sem = refs[-1]
    copies = [pltpu.make_async_copy(refs[i], refs[n + i], sem.at[i]) for i in range(n)]
    for c in copies:
        c.start()
    for c in copies:
        c.wait()


def grouped(sizes):
    groups = []
    for axis, n in zip(AXES, sizes):
        if groups and groups[-1][1] * n <= 32:
            groups[-1] = (groups[-1][0] + (axis,), groups[-1][1] * n)
        else:
            groups.append(((axis,), n))
    return groups


def kernel(cfg, q_hbm, k_hbm, v_hbm, s_hbm, g_hbm, qg_hbm, kg_hbm, seg_hbm,
           att_o, dq_o, dk_o, dv_o, gq_o, gk_o,
           qv, kv, vv, gv, s_ref, qg_ref, kg_ref, seg_ref, vd, near, give, take, gsrc, gslot,
           load_sem, send_sem, recv_sem, give_sem, take_sem, gsend, grecv):
    sizes, rows, heads, hd, h, hpc = cfg
    n_dp, n_blk, n_inner = sizes
    nc = heads // hpc
    hh = h // 2
    width = hpc * hd
    scale = 1.0 / math.sqrt(hd)
    blk, inner = lax.axis_index("blk"), lax.axis_index("inner")
    p = blk * n_inner + inner
    last = n_blk * n_inner - 1
    has_left, has_right = p > 0, p < last
    left, right = p - 1, p + 1

    size_of = dict(zip(AXES, sizes))
    stages = grouped(sizes)

    def place(axes):
        index = 0
        for axis in axes:
            index = index * size_of[axis] + lax.axis_index(axis)
        return index

    def member(axes, index):
        device = {}
        for axis in reversed(axes):
            device[axis] = lax.rem(index, size_of[axis])
            index = index // size_of[axis]
        return device

    def at(pos):
        return {"blk": pos // n_inner, "inner": lax.rem(pos, n_inner)}

    loads = [
        pltpu.make_async_copy(src, dst, load_sem.at[i])
        for i, (src, dst) in enumerate(((s_hbm, s_ref), (v_hbm, vv), (seg_hbm, seg_ref), (qg_hbm, qg_ref),
                                   (kg_hbm, kg_ref), (q_hbm, qv), (k_hbm, kv), (g_hbm, gv)))
    ]
    for c in loads:
        c.start()

    barrier = pltpu.get_barrier_semaphore()
    for axes, n in stages:
        me = place(axes)
        for d in range(1, n):
            pl.semaphore_signal(barrier, inc=1, device_id=member(axes, lax.rem(me + d, n)),
                                device_id_type=MESH)

    @pl.when(has_left)
    def _():
        pl.semaphore_signal(barrier, inc=1, device_id=at(left), device_id_type=MESH)

    @pl.when(has_right)
    def _():
        pl.semaphore_signal(barrier, inc=1, device_id=at(right), device_id_type=MESH)

    lane = lax.broadcasted_iota(jnp.int32, (rows, heads), 1)
    loads[0].wait()
    s_f = transposed(s_ref[...])

    def scale_of(head):
        return jnp.sum(jnp.where(lane == head, s_f, 0.0), axis=1, keepdims=True)

    loads[1].wait()
    for head in range(heads):
        cols = slice(head * hd, (head + 1) * hd)
        vd[:, cols] = (vv[:, cols].astype(F32) * s_f[:, head:head + 1]).astype(BF16)

    def seg_at(pos):
        start = pl.multiple_of(pos * rows, 128)
        return seg_ref[:, pl.ds(start, rows)].astype(F32)

    loads[2].wait()
    own = seg_at(p)
    prev = jnp.where(has_left, seg_at(jnp.maximum(left, 0)), -1.0)
    nxt = jnp.where(has_right, seg_at(jnp.minimum(right, last)), -2.0)
    own_col = to_column(own)
    edge = jnp.concatenate(
        [prev[:, rows - h:], own[:, :h], own[:, rows - h:], nxt[:, :h]], axis=1)
    edge_col = to_column(edge)
    wide_col = jnp.concatenate([to_column(prev)[rows - hh:], own_col, to_column(nxt)[:hh]], axis=0)
    same_own = wide_col == own

    def pick(row, index):
        return jnp.sum(row[:, index:index + 1], axis=1, keepdims=True)

    before, after = pick(prev, rows - 1), pick(nxt, 0)
    inside = jnp.where((own_col == before) | (own_col == after), 0.0, 1.0)
    split_lo = own_col[:h] == before
    split_hi = own_col[rows - h:] == after
    split_f = 1.0 - jnp.concatenate([inside[:h], inside[rows - h:]], axis=0)
    long_lo = jnp.where(pick(own, hh) == before, 1.0, 0.0)
    long_hi = jnp.where(pick(own, rows - hh - 1) == after, 1.0, 0.0)
    long_before = jnp.where(pick(prev, rows - hh - 1) == pick(own, 0), 1.0, 0.0)
    long_after = jnp.where(pick(nxt, hh) == pick(own, rows - 1), 1.0, 0.0)
    place_e = lax.broadcasted_iota(jnp.int32, (1, 4 * h), 1)
    asks = jnp.where(
        (place_e < hh) | (place_e >= 4 * h - hh), 0.0,
        jnp.where(place_e < h, 1.0 - long_before,
                  jnp.where(place_e >= 3 * h, 1.0 - long_after, 1.0)))
    same_edge = jnp.where(edge_col == edge, asks, 0.0) > 0.5
    lo_is_long = jnp.broadcast_to(long_lo, (hh, hd)) > 0.5
    hi_is_long = jnp.broadcast_to(long_hi, (hh, hd)) > 0.5
    lo_far = jnp.broadcast_to(own_col[hh:h], (hh, hd)) == before
    hi_far = jnp.broadcast_to(own_col[rows - h:rows - hh], (hh, hd)) == after
    lo_adds = jnp.where(own_col[:hh] == before, long_before, 0.0)
    hi_adds = jnp.where(own_col[rows - hh:] == after, long_after, 0.0)

    pl.semaphore_wait(barrier, sum(n - 1 for _, n in stages)
                      + has_left.astype(jnp.int32) + has_right.astype(jnp.int32))

    srcs = (k_hbm, vd)

    def columns(c):
        return pl.ds(pl.multiple_of(c * width, 128), width)

    def remote(side, i, c):
        own_rows = slice(0, hh) if side == 0 else slice(rows - hh, rows)
        cols = slice(c * width, (c + 1) * width)
        return pltpu.make_async_remote_copy(
            src_ref=srcs[i].at[own_rows, cols],
            dst_ref=near.at[i, 1 - side, :, cols],
            send_sem=send_sem.at[side, i, c],
            recv_sem=recv_sem.at[1 - side, i, c],
            device_id=at(left if side == 0 else right),
            device_id_type=MESH,
        )

    def receive(side, i, c):
        return pltpu.make_async_remote_copy(
            src_ref=near.at[i, side, :, columns(c)],
            dst_ref=near.at[i, side, :, columns(c)],
            send_sem=send_sem.at[side, i, c],
            recv_sem=recv_sem.at[side, i, c],
            device_id=at(left if side == 0 else right),
            device_id_type=MESH,
        )

    def second(side, c):
        return pltpu.make_async_remote_copy(
            src_ref=give.at[side, :, :, columns(c)],
            dst_ref=take.at[1 - side, :, :, columns(c)],
            send_sem=give_sem.at[side, c],
            recv_sem=take_sem.at[1 - side, c],
            device_id=at(left if side == 0 else right),
            device_id_type=MESH,
        )

    def second_receive(side, c):
        return pltpu.make_async_remote_copy(
            src_ref=take.at[side, :, :, columns(c)],
            dst_ref=take.at[side, :, :, columns(c)],
            send_sem=give_sem.at[side, c],
            recv_sem=take_sem.at[side, c],
            device_id=at(left if side == 0 else right),
            device_id_type=MESH,
        )

    sides = ((0, has_left), (1, has_right))
    for c in range(nc):
        for side, there in sides:
            @pl.when(there)
            def _():
                for i in range(2):
                    remote(side, i, c).start()

    for side, there in sides:
        @pl.when(jnp.logical_not(there))
        def _():
            near[:, side] = jnp.zeros((2, hh, heads * hd), BF16)
            take[side] = jnp.zeros((2, hh, heads * hd), BF16)

    for c in loads[3:]:
        c.wait()
    q_gain, k_gain = qg_ref[...], kg_ref[...]

    def own_step(c, acc):
        acc_q, acc_k = acc
        for side, there in sides:
            @pl.when(there)
            def _():
                for i in range(2):
                    receive(side, i, c).wait_recv()
        for j in range(hpc):
            head = c * hpc + j
            cols = pl.ds(pl.multiple_of(head * hd, 128), hd)
            q, g = qv[:, cols], gv[:, cols]
            k = jnp.concatenate([near[0, 0, :, cols], kv[:, cols], near[0, 1, :, cols]], axis=0)
            v = jnp.concatenate([near[1, 0, :, cols], vd[:, cols], near[1, 1, :, cols]], axis=0)
            k, v_f = k.astype(F32), v.astype(F32)
            q_f, g_f = q.astype(F32), g.astype(F32)
            q_unit, q_inv = unit(q_f)
            k_unit, k_inv = unit(k)
            out, d_q, d_k, d_v = attend(
                (q_unit * q_gain).astype(BF16), (k_unit * k_gain).astype(BF16),
                v, g, same_own, scale)
            far, beyond = slice(h, h + hh), slice(hh + rows, rows + h)
            give[0, 0, :, cols] = jnp.where(
                lo_is_long, jnp.where(lo_far, k[far], d_k[:hh]), q_f[:hh]).astype(BF16)
            give[0, 1, :, cols] = jnp.where(
                lo_is_long, jnp.where(lo_far, v_f[far], d_v[:hh]), g_f[:hh]).astype(BF16)
            far = slice(rows - hh, rows)
            give[1, 0, :, cols] = jnp.where(
                hi_is_long, jnp.where(hi_far, k[far], d_k[beyond]), q_f[rows - hh:]).astype(BF16)
            give[1, 1, :, cols] = jnp.where(
                hi_is_long, jnp.where(hi_far, v_f[far], d_v[beyond]), g_f[rows - hh:]).astype(BF16)
            mid = slice(hh, hh + rows)
            d_k, d_v, k_unit, k_inv = d_k[mid], d_v[mid], k_unit[mid], k_inv[mid]
            att_o[:, cols] = out.astype(BF16)
            dq_o[:, cols] = norm_back(d_q, q_unit, q_inv, q_gain).astype(BF16)
            dk_o[:, cols] = norm_back(d_k, k_unit, k_inv, k_gain).astype(BF16)
            dv_o[:, cols] = (d_v * scale_of(head)).astype(BF16)
            acc_q = acc_q + jnp.sum(jnp.where(inside > 0.5, d_q * q_unit, 0.0), axis=0, keepdims=True)
            acc_k = acc_k + jnp.sum(jnp.where(inside > 0.5, d_k * k_unit, 0.0), axis=0, keepdims=True)
        for side, there in sides:
            @pl.when(there)
            def _():
                second(side, c).start()
        return acc_q, acc_k

    zero = jnp.zeros((1, hd), F32)
    acc = lax.fori_loop(0, nc, own_step, (zero, zero))

    none = jnp.zeros((hh, hd), BF16)

    def joined(ref, cols, far_lo, near_lo, near_hi, far_hi):
        return jnp.concatenate(
            [far_lo, near_lo, ref[0:h, cols], ref[rows - h:rows, cols], near_hi, far_hi], axis=0)

    def put(ref, cols, value):
        ref[0:h, cols] = jnp.where(split_lo, value[:h].astype(F32),
                                   ref[0:h, cols].astype(F32)).astype(BF16)
        ref[rows - h:rows, cols] = jnp.where(split_hi, value[h:].astype(F32),
                                             ref[rows - h:rows, cols].astype(F32)).astype(BF16)

    def edge_step(c, acc):
        acc_q, acc_k = acc
        for side, there in sides:
            @pl.when(there)
            def _():
                second_receive(side, c).wait_recv()
        for j in range(hpc):
            head = c * hpc + j
            cols = pl.ds(pl.multiple_of(head * hd, 128), hd)
            lo_0, lo_1 = take[0, 0, :, cols], take[0, 1, :, cols]
            hi_0, hi_1 = take[1, 0, :, cols], take[1, 1, :, cols]
            q_unit, q_inv = unit(joined(qv, cols, none, lo_0, hi_0, none).astype(F32))
            k_unit, k_inv = unit(joined(
                kv, cols, lo_0, near[0, 0, :, cols], near[0, 1, :, cols], hi_0).astype(F32))
            out, d_q, d_k, d_v = attend(
                (q_unit * q_gain).astype(BF16), (k_unit * k_gain).astype(BF16),
                joined(vd, cols, lo_1, near[1, 0, :, cols], near[1, 1, :, cols], hi_1),
                joined(gv, cols, none, lo_1, hi_1, none), same_edge, scale)
            mid = slice(h, 3 * h)

            def with_sums(x, lo, hi):
                return jnp.concatenate(
                    [x[h:h + hh] + jnp.where(lo_adds > 0.5, lo.astype(F32), 0.0),
                     x[h + hh:3 * h - hh],
                     x[3 * h - hh:3 * h] + jnp.where(hi_adds > 0.5, hi.astype(F32), 0.0)], axis=0)

            d_v = with_sums(d_v, lo_1, hi_1)
            d_k = with_sums(d_k, lo_0, hi_0)
            d_q, q_unit, k_unit = d_q[mid], q_unit[mid], k_unit[mid]
            s_all = scale_of(head)
            s_mid = jnp.concatenate([s_all[:h], s_all[rows - h:]], axis=0)
            put(att_o, cols, out[mid])
            put(dq_o, cols, norm_back(d_q, q_unit, q_inv[mid], q_gain))
            put(dk_o, cols, norm_back(d_k, k_unit, k_inv[mid], k_gain))
            put(dv_o, cols, d_v * s_mid)
            acc_q = acc_q + jnp.sum(jnp.where(split_f > 0.5, d_q * q_unit, 0.0), axis=0, keepdims=True)
            acc_k = acc_k + jnp.sum(jnp.where(split_f > 0.5, d_k * k_unit, 0.0), axis=0, keepdims=True)
        return acc_q, acc_k

    acc_q, acc_k = lax.fori_loop(0, nc, edge_step, acc)

    total = jnp.concatenate([acc_q, acc_k], axis=0)
    offset = 0
    for stage, (axes, n) in enumerate(stages):
        me = place(axes)
        gsrc[stage] = total
        gslot[offset + me] = total

        def gain_copy(d, slot, to):
            return pltpu.make_async_remote_copy(
                src_ref=gsrc.at[stage], dst_ref=gslot.at[offset + slot],
                send_sem=gsend.at[offset + d], recv_sem=grecv.at[offset + d],
                device_id=member(axes, to), device_id_type=MESH)

        for d in range(1, n):
            gain_copy(d, me, lax.rem(me + d, n)).start()
        for d in range(1, n):
            gain_copy(d, lax.rem(me - d + n, n), lax.rem(me + d, n)).wait()
        total = gslot[offset]
        for i in range(1, n):
            total = total + gslot[offset + i]
        offset += n
    gq_o[...] = total[0:1]
    gk_o[...] = total[1:2]

    for c in range(nc):
        for side, there in sides:
            @pl.when(there)
            def _():
                for i in range(2):
                    remote(side, i, c).wait_send()
                second(side, c).wait_send()


def local(queries, keys, values, v_scale, d_out, q_gain, k_gain, segment_ids):
    _, rows, cols = queries.shape
    hd = q_gain.shape[0]
    heads = cols // hd
    sizes = tuple(lax.axis_size(a) for a in AXES)
    h = rows * sizes[2] // 8
    hpc = 3 if heads % 3 == 0 else 1
    nc = heads // hpc
    flat = lambda x: x.reshape(rows, x.shape[2])
    vmem = pl.BlockSpec(memory_space=pltpu.VMEM)
    hbm = pl.BlockSpec(memory_space=pltpu.HBM)
    big = jax.ShapeDtypeStruct((rows, cols), BF16)
    small = jax.ShapeDtypeStruct((1, hd), F32)
    slots = sum(n for _, n in grouped(sizes))
    outs = pl.pallas_call(
        functools.partial(kernel, (sizes, rows, heads, hd, h, hpc)),
        out_shape=(big, big, big, big, small, small),
        in_specs=[hbm] * 8,
        out_specs=(vmem,) * 6,
        scratch_shapes=[
            pltpu.VMEM((rows, cols), BF16),
            pltpu.VMEM((rows, cols), BF16),
            pltpu.VMEM((rows, cols), BF16),
            pltpu.VMEM((rows, cols), BF16),
            pltpu.VMEM((heads, rows), BF16),
            pltpu.VMEM((1, hd), F32),
            pltpu.VMEM((1, hd), F32),
            pltpu.VMEM(segment_ids.shape, jnp.int32),
            pltpu.VMEM((rows, cols), BF16),
            pltpu.VMEM((2, 2, h // 2, cols), BF16),
            pltpu.VMEM((2, 2, h // 2, cols), BF16),
            pltpu.VMEM((2, 2, h // 2, cols), BF16),
            pltpu.VMEM((3, 2, hd), F32),
            pltpu.VMEM((slots, 2, hd), F32),
            pltpu.SemaphoreType.DMA((8,)),
            pltpu.SemaphoreType.DMA((2, 2, nc)),
            pltpu.SemaphoreType.DMA((2, 2, nc)),
            pltpu.SemaphoreType.DMA((2, nc)),
            pltpu.SemaphoreType.DMA((2, nc)),
            pltpu.SemaphoreType.DMA((slots,)),
            pltpu.SemaphoreType.DMA((slots,)),
        ],
        compiler_params=pltpu.CompilerParams(
            collective_id=0, has_side_effects=True, vmem_limit_bytes=32 << 20),
    )(*map(lambda x: pltpu.with_memory_space_constraint(x, pltpu.HBM), (flat(queries), flat(keys), flat(values), flat(v_scale).T, flat(d_out),
      q_gain.reshape(1, hd), k_gain.reshape(1, hd), segment_ids)))
    outs = pl.pallas_call(
        store,
        out_shape=(big, big, big, big, small, small),
        in_specs=[vmem] * 6,
        out_specs=(hbm,) * 6,
        scratch_shapes=[pltpu.SemaphoreType.DMA((6,))],
    )(*map(lambda x: pltpu.with_memory_space_constraint(x, pltpu.VMEM), outs))
    wide = tuple(x.reshape(1, rows, cols) for x in outs[:4])
    return wide + (outs[4].reshape(hd), outs[5].reshape(hd))


def solution(mesh):
    tokens = P("dp", ("blk", "inner"), None)
    return jax.shard_map(
        local,
        mesh=mesh,
        in_specs=(tokens,) * 5 + (P(), P(), P("dp", None)),
        out_specs=(tokens,) * 4 + (P(), P()),
        check_vma=False,
    )
```

```python
import functools
import math

import jax
import jax.numpy as jnp
from jax import lax
from jax.experimental import pallas as pl
from jax.experimental.pallas import tpu as pltpu
from jax.sharding import PartitionSpec as P

EPSILON = 1e-06
MESH = pl.DeviceIdType.MESH
AXES = ("dp", "blk", "inner")
F32 = jnp.float32
BF16 = jnp.bfloat16
NT = (((1,), (1,)), ((), ()))
NN = (((1,), (0,)), ((), ()))
TN = (((0,), (0,)), ((), ()))


def dot(a, b, dims):
    return lax.dot_general(a, b, dims, preferred_element_type=F32)


def unit(x):
    inverse = lax.rsqrt(jnp.mean(x * x, axis=-1, keepdims=True) + EPSILON)
    return x * inverse, inverse


def norm_back(d_norm, unit_rows, inverse, gain):
    d_unit = d_norm * gain
    mean = jnp.mean(d_unit * unit_rows, axis=-1, keepdims=True)
    return inverse * (d_unit - unit_rows * mean)


def attend(q_norm, k_norm, v_deq, grad, same, scale):
    e = jnp.where(same, jnp.exp(dot(k_norm, q_norm, NT) * scale), 0.0)
    total = jnp.sum(e, axis=0, keepdims=True)
    w = e * (1.0 / jnp.where(total == 0.0, 1.0, total))
    w_b = w.astype(BF16)
    d_w = dot(v_deq, grad, NT)
    out_dot = jnp.sum(w * d_w, axis=0, keepdims=True)
    d_s = (w * (d_w - out_dot)).astype(BF16)
    return (
        dot(w_b, v_deq, TN),
        dot(d_s, k_norm, TN) * scale,
        dot(d_s, q_norm, NN) * scale,
        dot(w_b, grad, NN),
    )


def to_column(row):
    n = row.shape[1]
    r = lax.broadcasted_iota(jnp.int32, (n, n), 0)
    c = lax.broadcasted_iota(jnp.int32, (n, n), 1)
    return jnp.sum(jnp.where(r == c, row, 0.0), axis=1, keepdims=True)


def transposed(x):
    n = x.shape[1]
    r = lax.broadcasted_iota(jnp.int32, (n, n), 0)
    c = lax.broadcasted_iota(jnp.int32, (n, n), 1)
    return dot((r == c).astype(F32).astype(BF16), x, NT)


def store(*refs):
    n = len(refs) // 2
    sem = refs[-1]
    copies = [pltpu.make_async_copy(refs[i], refs[n + i], sem.at[i]) for i in range(n)]
    for c in copies:
        c.start()
    for c in copies:
        c.wait()


def grouped(sizes):
    groups = []
    for axis, n in zip(AXES, sizes):
        if groups and groups[-1][1] * n <= 32:
            groups[-1] = (groups[-1][0] + (axis,), groups[-1][1] * n)
        else:
            groups.append(((axis,), n))
    return groups


def kernel(cfg, q_hbm, k_hbm, v_hbm, s_hbm, g_hbm, qg_hbm, kg_hbm, seg_hbm,
           att_o, dq_o, dk_o, dv_o, gq_o, gk_o,
           qv, kv, vv, gv, s_ref, qg_ref, kg_ref, seg_ref, vd, near, give, take, gsrc, gslot,
           load_sem, send_sem, recv_sem, give_sem, take_sem, gsend, grecv):
    sizes, rows, heads, hd, h, hpc = cfg
    n_dp, n_blk, n_inner = sizes
    nc = heads // hpc
    hh = h // 2
    width = hpc * hd
    scale = 1.0 / math.sqrt(hd)
    blk, inner = lax.axis_index("blk"), lax.axis_index("inner")
    p = blk * n_inner + inner
    last = n_blk * n_inner - 1
    has_left, has_right = p > 0, p < last
    left, right = p - 1, p + 1

    size_of = dict(zip(AXES, sizes))
    stages = grouped(sizes)

    def place(axes):
        index = 0
        for axis in axes:
            index = index * size_of[axis] + lax.axis_index(axis)
        return index

    def member(axes, index):
        device = {}
        for axis in reversed(axes):
            device[axis] = lax.rem(index, size_of[axis])
            index = index // size_of[axis]
        return device

    def at(pos):
        return {"blk": pos // n_inner, "inner": lax.rem(pos, n_inner)}

    loads = [
        pltpu.make_async_copy(src, dst, load_sem.at[i])
        for i, (src, dst) in enumerate(((s_hbm, s_ref), (v_hbm, vv), (seg_hbm, seg_ref), (qg_hbm, qg_ref),
                                   (kg_hbm, kg_ref), (q_hbm, qv), (k_hbm, kv), (g_hbm, gv)))
    ]
    for c in loads:
        c.start()

    barrier = pltpu.get_barrier_semaphore()
    for axes, n in stages:
        me = place(axes)
        for d in range(1, n):
            pl.semaphore_signal(barrier, inc=1, device_id=member(axes, lax.rem(me + d, n)),
                                device_id_type=MESH)

    @pl.when(has_left)
    def _():
        pl.semaphore_signal(barrier, inc=1, device_id=at(left), device_id_type=MESH)

    @pl.when(has_right)
    def _():
        pl.semaphore_signal(barrier, inc=1, device_id=at(right), device_id_type=MESH)

    lane = lax.broadcasted_iota(jnp.int32, (rows, heads), 1)
    loads[0].wait()
    s_f = transposed(s_ref[...])

    def scale_of(head):
        return jnp.sum(jnp.where(lane == head, s_f, 0.0), axis=1, keepdims=True)

    loads[1].wait()
    for head in range(heads):
        cols = slice(head * hd, (head + 1) * hd)
        vd[:, cols] = (vv[:, cols].astype(F32) * s_f[:, head:head + 1]).astype(BF16)

    def seg_at(pos):
        start = pl.multiple_of(pos * rows, 128)
        return seg_ref[:, pl.ds(start, rows)].astype(F32)

    loads[2].wait()
    own = seg_at(p)
    prev = jnp.where(has_left, seg_at(jnp.maximum(left, 0)), -1.0)
    nxt = jnp.where(has_right, seg_at(jnp.minimum(right, last)), -2.0)
    own_col = to_column(own)
    edge = jnp.concatenate(
        [prev[:, rows - h:], own[:, :h], own[:, rows - h:], nxt[:, :h]], axis=1)
    edge_col = to_column(edge)
    wide_col = jnp.concatenate([to_column(prev)[rows - hh:], own_col, to_column(nxt)[:hh]], axis=0)
    same_own = wide_col == own

    def pick(row, index):
        return jnp.sum(row[:, index:index + 1], axis=1, keepdims=True)

    before, after = pick(prev, rows - 1), pick(nxt, 0)
    inside = jnp.where((own_col == before) | (own_col == after), 0.0, 1.0)
    split_lo = own_col[:h] == before
    split_hi = own_col[rows - h:] == after
    split_f = 1.0 - jnp.concatenate([inside[:h], inside[rows - h:]], axis=0)
    long_lo = jnp.where(pick(own, hh) == before, 1.0, 0.0)
    long_hi = jnp.where(pick(own, rows - hh - 1) == after, 1.0, 0.0)
    long_before = jnp.where(pick(prev, rows - hh - 1) == pick(own, 0), 1.0, 0.0)
    long_after = jnp.where(pick(nxt, hh) == pick(own, rows - 1), 1.0, 0.0)
    place_e = lax.broadcasted_iota(jnp.int32, (1, 4 * h), 1)
    asks = jnp.where(
        (place_e < hh) | (place_e >= 4 * h - hh), 0.0,
        jnp.where(place_e < h, 1.0 - long_before,
                  jnp.where(place_e >= 3 * h, 1.0 - long_after, 1.0)))
    same_edge = jnp.where(edge_col == edge, asks, 0.0) > 0.5
    lo_is_long = jnp.broadcast_to(long_lo, (hh, hd)) > 0.5
    hi_is_long = jnp.broadcast_to(long_hi, (hh, hd)) > 0.5
    lo_far = jnp.broadcast_to(own_col[hh:h], (hh, hd)) == before
    hi_far = jnp.broadcast_to(own_col[rows - h:rows - hh], (hh, hd)) == after
    lo_adds = jnp.where(own_col[:hh] == before, long_before, 0.0)
    hi_adds = jnp.where(own_col[rows - hh:] == after, long_after, 0.0)

    pl.semaphore_wait(barrier, sum(n - 1 for _, n in stages)
                      + has_left.astype(jnp.int32) + has_right.astype(jnp.int32))

    srcs = (k_hbm, vd)

    def columns(c):
        return pl.ds(pl.multiple_of(c * width, 128), width)

    def remote(side, i, c):
        own_rows = slice(0, hh) if side == 0 else slice(rows - hh, rows)
        cols = slice(c * width, (c + 1) * width)
        return pltpu.make_async_remote_copy(
            src_ref=srcs[i].at[own_rows, cols],
            dst_ref=near.at[i, 1 - side, :, cols],
            send_sem=send_sem.at[side, i, c],
            recv_sem=recv_sem.at[1 - side, i, c],
            device_id=at(left if side == 0 else right),
            device_id_type=MESH,
        )

    def receive(side, i, c):
        return pltpu.make_async_remote_copy(
            src_ref=near.at[i, side, :, columns(c)],
            dst_ref=near.at[i, side, :, columns(c)],
            send_sem=send_sem.at[side, i, c],
            recv_sem=recv_sem.at[side, i, c],
            device_id=at(left if side == 0 else right),
            device_id_type=MESH,
        )

    def second(side, c):
        return pltpu.make_async_remote_copy(
            src_ref=give.at[side, :, :, columns(c)],
            dst_ref=take.at[1 - side, :, :, columns(c)],
            send_sem=give_sem.at[side, c],
            recv_sem=take_sem.at[1 - side, c],
            device_id=at(left if side == 0 else right),
            device_id_type=MESH,
        )

    def second_receive(side, c):
        return pltpu.make_async_remote_copy(
            src_ref=take.at[side, :, :, columns(c)],
            dst_ref=take.at[side, :, :, columns(c)],
            send_sem=give_sem.at[side, c],
            recv_sem=take_sem.at[side, c],
            device_id=at(left if side == 0 else right),
            device_id_type=MESH,
        )

    sides = ((0, has_left), (1, has_right))
    for c in range(nc):
        for side, there in sides:
            @pl.when(there)
            def _():
                for i in range(2):
                    remote(side, i, c).start()

    for side, there in sides:
        @pl.when(jnp.logical_not(there))
        def _():
            near[:, side] = jnp.zeros((2, hh, heads * hd), BF16)
            take[side] = jnp.zeros((2, hh, heads * hd), BF16)

    for c in loads[3:]:
        c.wait()
    q_gain, k_gain = qg_ref[...], kg_ref[...]

    def own_step(c, acc):
        acc_q, acc_k = acc
        for side, there in sides:
            @pl.when(there)
            def _():
                for i in range(2):
                    receive(side, i, c).wait_recv()
        for j in range(hpc):
            head = c * hpc + j
            cols = pl.ds(pl.multiple_of(head * hd, 128), hd)
            q, g = qv[:, cols], gv[:, cols]
            k = jnp.concatenate([near[0, 0, :, cols], kv[:, cols], near[0, 1, :, cols]], axis=0)
            v = jnp.concatenate([near[1, 0, :, cols], vd[:, cols], near[1, 1, :, cols]], axis=0)
            k, v_f = k.astype(F32), v.astype(F32)
            q_f, g_f = q.astype(F32), g.astype(F32)
            q_unit, q_inv = unit(q_f)
            k_unit, k_inv = unit(k)
            out, d_q, d_k, d_v = attend(
                (q_unit * q_gain).astype(BF16), (k_unit * k_gain).astype(BF16),
                v, g, same_own, scale)
            far, beyond = slice(h, h + hh), slice(hh + rows, rows + h)
            give[0, 0, :, cols] = jnp.where(
                lo_is_long, jnp.where(lo_far, k[far], d_k[:hh]), q_f[:hh]).astype(BF16)
            give[0, 1, :, cols] = jnp.where(
                lo_is_long, jnp.where(lo_far, v_f[far], d_v[:hh]), g_f[:hh]).astype(BF16)
            far = slice(rows - hh, rows)
            give[1, 0, :, cols] = jnp.where(
                hi_is_long, jnp.where(hi_far, k[far], d_k[beyond]), q_f[rows - hh:]).astype(BF16)
            give[1, 1, :, cols] = jnp.where(
                hi_is_long, jnp.where(hi_far, v_f[far], d_v[beyond]), g_f[rows - hh:]).astype(BF16)
            mid = slice(hh, hh + rows)
            d_k, d_v, k_unit, k_inv = d_k[mid], d_v[mid], k_unit[mid], k_inv[mid]
            att_o[:, cols] = out.astype(BF16)
            dq_o[:, cols] = norm_back(d_q, q_unit, q_inv, q_gain).astype(BF16)
            dk_o[:, cols] = norm_back(d_k, k_unit, k_inv, k_gain).astype(BF16)
            dv_o[:, cols] = (d_v * scale_of(head)).astype(BF16)
            acc_q = acc_q + jnp.sum(jnp.where(inside > 0.5, d_q * q_unit, 0.0), axis=0, keepdims=True)
            acc_k = acc_k + jnp.sum(jnp.where(inside > 0.5, d_k * k_unit, 0.0), axis=0, keepdims=True)
        for side, there in sides:
            @pl.when(there)
            def _():
                second(side, c).start()
        return acc_q, acc_k

    zero = jnp.zeros((1, hd), F32)
    acc = lax.fori_loop(0, nc, own_step, (zero, zero))

    none = jnp.zeros((hh, hd), BF16)

    def joined(ref, cols, far_lo, near_lo, near_hi, far_hi):
        return jnp.concatenate(
            [far_lo, near_lo, ref[0:h, cols], ref[rows - h:rows, cols], near_hi, far_hi], axis=0)

    def put(ref, cols, value):
        ref[0:h, cols] = jnp.where(split_lo, value[:h].astype(F32),
                                   ref[0:h, cols].astype(F32)).astype(BF16)
        ref[rows - h:rows, cols] = jnp.where(split_hi, value[h:].astype(F32),
                                             ref[rows - h:rows, cols].astype(F32)).astype(BF16)

    def edge_step(c, acc):
        acc_q, acc_k = acc
        for side, there in sides:
            @pl.when(there)
            def _():
                second_receive(side, c).wait_recv()
        for j in range(hpc):
            head = c * hpc + j
            cols = pl.ds(pl.multiple_of(head * hd, 128), hd)
            lo_0, lo_1 = take[0, 0, :, cols], take[0, 1, :, cols]
            hi_0, hi_1 = take[1, 0, :, cols], take[1, 1, :, cols]
            q_unit, q_inv = unit(joined(qv, cols, none, lo_0, hi_0, none).astype(F32))
            k_unit, k_inv = unit(joined(
                kv, cols, lo_0, near[0, 0, :, cols], near[0, 1, :, cols], hi_0).astype(F32))
            out, d_q, d_k, d_v = attend(
                (q_unit * q_gain).astype(BF16), (k_unit * k_gain).astype(BF16),
                joined(vd, cols, lo_1, near[1, 0, :, cols], near[1, 1, :, cols], hi_1),
                joined(gv, cols, none, lo_1, hi_1, none), same_edge, scale)
            mid = slice(h, 3 * h)

            def with_sums(x, lo, hi):
                return jnp.concatenate(
                    [x[h:h + hh] + jnp.where(lo_adds > 0.5, lo.astype(F32), 0.0),
                     x[h + hh:3 * h - hh],
                     x[3 * h - hh:3 * h] + jnp.where(hi_adds > 0.5, hi.astype(F32), 0.0)], axis=0)

            d_v = with_sums(d_v, lo_1, hi_1)
            d_k = with_sums(d_k, lo_0, hi_0)
            d_q, q_unit, k_unit = d_q[mid], q_unit[mid], k_unit[mid]
            s_all = scale_of(head)
            s_mid = jnp.concatenate([s_all[:h], s_all[rows - h:]], axis=0)
            put(att_o, cols, out[mid])
            put(dq_o, cols, norm_back(d_q, q_unit, q_inv[mid], q_gain))
            put(dk_o, cols, norm_back(d_k, k_unit, k_inv[mid], k_gain))
            put(dv_o, cols, d_v * s_mid)
            acc_q = acc_q + jnp.sum(jnp.where(split_f > 0.5, d_q * q_unit, 0.0), axis=0, keepdims=True)
            acc_k = acc_k + jnp.sum(jnp.where(split_f > 0.5, d_k * k_unit, 0.0), axis=0, keepdims=True)
        return acc_q, acc_k

    acc_q, acc_k = lax.fori_loop(0, nc, edge_step, acc)

    total = jnp.concatenate([acc_q, acc_k], axis=0)
    offset = 0
    for stage, (axes, n) in enumerate(stages):
        me = place(axes)
        gsrc[stage] = total
        gslot[offset + me] = total

        def gain_copy(d, slot, to):
            return pltpu.make_async_remote_copy(
                src_ref=gsrc.at[stage], dst_ref=gslot.at[offset + slot],
                send_sem=gsend.at[stage], recv_sem=grecv.at[stage],
                device_id=member(axes, to), device_id_type=MESH)

        for d in range(1, n):
            gain_copy(d, me, lax.rem(me + d, n)).start()
        everything = gslot.at[pl.ds(offset, n - 1)]
        pltpu.make_async_remote_copy(
            src_ref=everything, dst_ref=everything,
            send_sem=gsend.at[stage], recv_sem=grecv.at[stage],
            device_id=member(axes, lax.rem(me + 1, n)), device_id_type=MESH).wait()
        total = gslot[offset]
        for i in range(1, n):
            total = total + gslot[offset + i]
        offset += n
    gq_o[...] = total[0:1]
    gk_o[...] = total[1:2]

    for c in range(nc):
        for side, there in sides:
            @pl.when(there)
            def _():
                for i in range(2):
                    remote(side, i, c).wait_send()
                second(side, c).wait_send()


def local(queries, keys, values, v_scale, d_out, q_gain, k_gain, segment_ids):
    _, rows, cols = queries.shape
    hd = q_gain.shape[0]
    heads = cols // hd
    sizes = tuple(lax.axis_size(a) for a in AXES)
    h = rows * sizes[2] // 8
    hpc = 3 if heads % 3 == 0 else 1
    nc = heads // hpc
    flat = lambda x: x.reshape(rows, x.shape[2])
    vmem = pl.BlockSpec(memory_space=pltpu.VMEM)
    hbm = pl.BlockSpec(memory_space=pltpu.HBM)
    big = jax.ShapeDtypeStruct((rows, cols), BF16)
    small = jax.ShapeDtypeStruct((1, hd), F32)
    slots = sum(n for _, n in grouped(sizes))
    outs = pl.pallas_call(
        functools.partial(kernel, (sizes, rows, heads, hd, h, hpc)),
        out_shape=(big, big, big, big, small, small),
        in_specs=[hbm] * 8,
        out_specs=(vmem,) * 6,
        scratch_shapes=[
            pltpu.VMEM((rows, cols), BF16),
            pltpu.VMEM((rows, cols), BF16),
            pltpu.VMEM((rows, cols), BF16),
            pltpu.VMEM((rows, cols), BF16),
            pltpu.VMEM((heads, rows), BF16),
            pltpu.VMEM((1, hd), F32),
            pltpu.VMEM((1, hd), F32),
            pltpu.VMEM(segment_ids.shape, jnp.int32),
            pltpu.VMEM((rows, cols), BF16),
            pltpu.VMEM((2, 2, h // 2, cols), BF16),
            pltpu.VMEM((2, 2, h // 2, cols), BF16),
            pltpu.VMEM((2, 2, h // 2, cols), BF16),
            pltpu.VMEM((3, 2, hd), F32),
            pltpu.VMEM((slots, 2, hd), F32),
            pltpu.SemaphoreType.DMA((8,)),
            pltpu.SemaphoreType.DMA((2, 2, nc)),
            pltpu.SemaphoreType.DMA((2, 2, nc)),
            pltpu.SemaphoreType.DMA((2, nc)),
            pltpu.SemaphoreType.DMA((2, nc)),
            pltpu.SemaphoreType.DMA((slots,)),
            pltpu.SemaphoreType.DMA((slots,)),
        ],
        compiler_params=pltpu.CompilerParams(
            collective_id=0, has_side_effects=True, vmem_limit_bytes=32 << 20),
    )(*map(lambda x: pltpu.with_memory_space_constraint(x, pltpu.HBM), (flat(queries), flat(keys), flat(values), flat(v_scale).T, flat(d_out),
      q_gain.reshape(1, hd), k_gain.reshape(1, hd), segment_ids)))
    outs = pl.pallas_call(
        store,
        out_shape=(big, big, big, big, small, small),
        in_specs=[vmem] * 6,
        out_specs=(hbm,) * 6,
        scratch_shapes=[pltpu.SemaphoreType.DMA((6,))],
    )(*map(lambda x: pltpu.with_memory_space_constraint(x, pltpu.VMEM), outs))
    wide = tuple(x.reshape(1, rows, cols) for x in outs[:4])
    return wide + (outs[4].reshape(hd), outs[5].reshape(hd))


def solution(mesh):
    tokens = P("dp", ("blk", "inner"), None)
    return jax.shard_map(
        local,
        mesh=mesh,
        in_specs=(tokens,) * 5 + (P(), P(), P("dp", None)),
        out_specs=(tokens,) * 4 + (P(), P()),
        check_vma=False,
    )
```
